32 devices in a mesh: groups: 2 (over y), frame: 4 (over z), panel: 2 (over x), sub: 2 (over core).
Axes of the slice: x: 2, y: 2, z: 4, core: 2. Of those that a mesh axis runs over, the one named last changes fastest.
Arguments:
- frames: bfloat16 [2048, 65536], P(('groups', 'frame'), ('panel', 'sub')), parts along dimension 0, may hold values from -16 to 16
- slices: float32 [32, 65536], P(('groups', 'frame'), ('panel', 'sub')), parts along dimension 0, may hold values from -8 to 8
- log_prior: float32 [4096], replicated, may hold values from -2 to 2
- orient: int32 [32], P('groups'), parts along dimension 0, may hold values from 0 to 4095
Outputs:
- new_slices: float32 [32, 65536], P(('groups', 'frame'), ('panel', 'sub')), parts along dimension 0
The draws below stay inside these ranges and needn't reach their ends.
There are 2 independent parts, one for each index of `groups`. The reference program is written for one: setup_inputs(seed, part) draws one part's arguments, and reference() takes and returns one part's arrays. A program takes and returns all parts, laid end to end along the dimension named above; an argument that names none is the same for every part. Nothing has to cross between parts.
All inputs are finite; a program needn't handle non-finite values.
Results may differ from the reference program's by a relative error of at most 0.022.
The reference program's roundings to bfloat16 on the way (of `rounded` and `weights`) count: a program that leaves them out, or rounds other values in their place, can miss the bound.
Values may be sent and summed in bfloat16 or wider, within the bound.
A program may use at most 64 MiB of HBM per device.

```python
import math
import jax
import jax.numpy as jnp
from jax import lax

PIX = 65536
FRAMES_DEV = 256
NORIENT = 4096
ITERS = 2
FRAMES = 1024
SLICES = 16
N_FRAME = 4


def pixel_scale(key):
    lower = 0.5
    upper = 2.0
    unit = jax.random.uniform(jax.random.fold_in(key, 31), (PIX,), jnp.float32)
    return lower * jnp.exp(unit * math.log(upper / lower))


def unit_entries(key, shape):
    return jax.random.truncated_normal(key, -4.0, 4.0, shape, jnp.float32)


def slice_values(key):
    scale = pixel_scale(key)
    return unit_entries(jax.random.fold_in(key, 32), (SLICES, PIX)) * scale[None, :]


def draw_slices(key, part):
    return slice_values(key)


def draw_frames(key, part):
    source = slice_values(key)
    scale = pixel_scale(key)
    chosen = jax.random.randint(jax.random.fold_in(key, 33), (FRAMES,), 0, SLICES)
    level = jax.random.uniform(jax.random.fold_in(key, 34), (FRAMES,), jnp.float32)
    signal = jnp.exp(level * math.log(4.0)) / math.sqrt(PIX)
    noise = unit_entries(jax.random.fold_in(key, 35), (FRAMES, PIX)) * scale[None, :]
    picked = source[chosen]
    result = signal[:, None] * picked + noise
    return result.astype(jnp.bfloat16)


def set_ends(drawn, rng, least, largest):
    spot = [jax.random.randint(jax.random.fold_in(rng, axis), (), 0, length) for axis, length in enumerate(drawn.shape)]
    widest = drawn.shape.index(max(drawn.shape))
    beside = spot[:widest] + [(spot[widest] + 1) % drawn.shape[widest]] + spot[widest + 1:]
    return drawn.at[tuple(spot)].set(least).at[tuple(beside)].set(largest)


def setup_inputs(seed: int = 0, part: int = 0) -> dict:
    keys = jax.random.split(jax.random.key(seed), 5)
    part_keys = jax.random.split(jax.random.fold_in(keys[4], part), 5)
    return {
        "frames": draw_frames(jax.random.fold_in(jax.random.fold_in(keys[4], part), 71), part),
        "slices": draw_slices(jax.random.fold_in(jax.random.fold_in(keys[4], part), 71), part),
        "log_prior": jnp.clip(jax.random.uniform(keys[2], (NORIENT,), jnp.float32, -2.0, 2.0), -2.0, 2.0),
        "orient": set_ends(jax.random.randint(part_keys[3], (SLICES,), 0, NORIENT), jax.random.fold_in(part_keys[3], 1), 0, NORIENT - 1).astype(jnp.int32),
    }


def reference(frames, slices, log_prior, orient):
    prior = log_prior[orient]
    temper = 3.0 / math.sqrt(PIX)
    blocks = frames.reshape(N_FRAME, FRAMES_DEV, PIX)
    current = slices
    for step in range(ITERS):
        rounded = current.astype(jnp.bfloat16)
        wide = rounded.astype(jnp.float32)
        norms = lax.optimization_barrier(jnp.sum(wide * wide, axis=1))
        raw = jnp.dot(frames, rounded.T, preferred_element_type=jnp.float32) - 0.5 * norms[None, :]
        scores = temper * raw + prior[None, :]
        weights = jax.nn.softmax(scores, axis=1).astype(jnp.bfloat16)
        counts = lax.optimization_barrier(jnp.sum(weights.astype(jnp.float32), axis=0))
        weight_blocks = weights.reshape(N_FRAME, FRAMES_DEV, SLICES)

        def add_block(total, pair):
            block_w, block_f = pair
            term = jnp.dot(block_w.T, block_f, preferred_element_type=jnp.float32)
            term = lax.optimization_barrier(term.astype(jnp.bfloat16))
            return (total + term.astype(jnp.float32), None)
        totals, _ = lax.scan(add_block, jnp.zeros((SLICES, PIX), jnp.float32), (weight_blocks, blocks))
        current = (totals + wide) / (counts + 1.0)[:, None]
    return current
```

```python
import functools
import math

import jax
import jax.numpy as jnp
from jax import lax
from jax.experimental import pallas as pl
from jax.experimental.pallas import tpu as pltpu
from jax.sharding import PartitionSpec as P

ITERS = 2
CHUNK = 1024
SKEW = 2
MESH = pl.DeviceIdType.MESH


def kernel(
    sizes, frames_ref, slices_ref, prior_ref, orient_ref, out_ref,
    fv, sv, model, term, from_left, from_right, to_right, to_left,
    raws, counts, raw_acc, norm_acc, weights,
    frame_sem, slice_sem, right_send, right_recv, left_send, left_recv,
    raw_send, raw_recv, count_send, count_recv,
):
    n, panels, subs = sizes
    group = panels * subs
    z = lax.axis_index("frame")
    me = lax.axis_index("panel") * subs + lax.axis_index("sub")
    n_chunks, n_frames, width = fv.shape
    owned = slices_ref.shape[0]
    rows = model.shape[1]
    temper = 3.0 / math.sqrt(n_chunks * width * group)
    right, left = lax.rem(z + 1, n), lax.rem(z + n - 1, n)
    first, last = z == 0, z == n - 1

    slice_copy = pltpu.make_async_copy(slices_ref, sv, slice_sem)
    slice_copy.start()

    def frame_copy(c):
        start = pl.multiple_of(c * width, width)
        return pltpu.make_async_copy(frames_ref.at[:, pl.ds(start, width)], fv.at[c], frame_sem.at[c])

    @pl.loop(0, n_chunks)
    def _(c):
        frame_copy(c).start()

    def group_peer(k):
        other = lax.rem(me + k, group)
        return {"panel": other // subs, "sub": lax.rem(other, subs)}

    def frame_peer(k):
        return {"frame": lax.rem(z + k, n)}

    barrier = pltpu.get_barrier_semaphore()
    for k in range(1, group):
        pl.semaphore_signal(barrier, inc=1, device_id=group_peer(k), device_id_type=MESH)
    for k in range(1, n):
        pl.semaphore_signal(barrier, inc=1, device_id=frame_peer(k), device_id_type=MESH)

    slice_copy.wait()
    row = lax.broadcasted_iota(jnp.int32, (rows, 1), 0)
    prior = lax.fori_loop(
        0, rows, lambda m, v: jnp.where(row == m, prior_ref[orient_ref[m]], v), jnp.zeros((rows, 1), jnp.float32)
    )

    pl.semaphore_wait(barrier, group + n - 2)

    def right_copy(p, c):
        return pltpu.make_async_remote_copy(
            to_right.at[p, c], from_left.at[p, c], right_send.at[p, c], right_recv.at[p, c],
            device_id={"frame": right}, device_id_type=MESH,
        )

    def left_copy(p, c):
        return pltpu.make_async_remote_copy(
            to_left.at[p, c], from_right.at[p, c], left_send.at[p, c], left_recv.at[p, c],
            device_id={"frame": left}, device_id_type=MESH,
        )

    def raw_copy(it, k, slot):
        return pltpu.make_async_remote_copy(
            raws.at[it, me], raws.at[it, slot], raw_send.at[it, k], raw_recv.at[it, slot],
            device_id=group_peer(k), device_id_type=MESH,
        )

    def count_copy(it, k, slot):
        return pltpu.make_async_remote_copy(
            counts.at[it, z], counts.at[it, slot], count_send.at[it, k], count_recv.at[it, slot],
            device_id=frame_peer(k), device_id_type=MESH,
        )

    def sweep(p, make_term, combine):
        def step(s, _):
            @pl.when(s < n_chunks)
            def _():
                term[s] = make_term(s)

            c_right = s - z * SKEW

            @pl.when((c_right >= 0) & (c_right < n_chunks))
            def _():
                @pl.when(z > 0)
                def _():
                    right_copy(p, c_right).wait_recv()

                @pl.when(z < n - 1)
                def _():
                    came = jnp.where(first, 0.0, from_left[p, c_right].astype(jnp.float32))
                    to_right[p, c_right] = (came + term[c_right].astype(jnp.float32)).astype(jnp.bfloat16)
                    right_copy(p, c_right).start()

            c_left = s - (n - 1 - z) * SKEW

            @pl.when((c_left >= 0) & (c_left < n_chunks))
            def _():
                @pl.when(z < n - 1)
                def _():
                    left_copy(p, c_left).wait_recv()

                @pl.when(z > 0)
                def _():
                    came = jnp.where(last, 0.0, from_right[p, c_left].astype(jnp.float32))
                    to_left[p, c_left] = (came + term[c_left].astype(jnp.float32)).astype(jnp.bfloat16)
                    left_copy(p, c_left).start()

            c = s - jnp.maximum(z, n - 1 - z) * SKEW

            @pl.when((c >= 0) & (c < n_chunks))
            def _():
                low = jnp.where(first, 0.0, from_left[p, c].astype(jnp.float32))
                high = jnp.where(last, 0.0, from_right[p, c].astype(jnp.float32))
                combine(c, low + term[c].astype(jnp.float32) + high)

            return 0

        lax.fori_loop(0, n_chunks + (n - 1) * SKEW, step, 0)

    def score(c, rounded):
        model[c] = rounded
        wide = rounded.astype(jnp.float32)
        norm_acc[...] += jnp.sum(wide * wide, axis=1, keepdims=True)
        raw_acc[...] += lax.dot_general(
            rounded, fv[c], (((1,), (1,)), ((), ())), preferred_element_type=jnp.float32
        )

    def clear():
        raw_acc[...] = jnp.zeros_like(raw_acc)
        norm_acc[...] = jnp.zeros_like(norm_acc)

    def expect(it):
        raws[it, me] = raw_acc[...] - 0.5 * norm_acc[...]
        for k in range(1, group):
            raw_copy(it, k, me).start()
        for k in range(1, group):
            raw_copy(it, k, lax.rem(me + group - k, group)).wait_recv()
        summed = raws[it, 0]
        for j in range(1, group):
            summed = summed + raws[it, j]
        scores = temper * summed + prior
        top = jnp.exp(scores - jnp.max(scores, axis=0, keepdims=True))
        w = (top / jnp.sum(top, axis=0, keepdims=True)).astype(jnp.bfloat16)
        weights[...] = w
        mine = jnp.sum(w.astype(jnp.float32), axis=1, keepdims=True)
        counts[it, z] = jnp.broadcast_to(mine, counts.shape[2:])

        @pl.loop(1, n)
        def _(k):
            count_copy(it, k, z).start()

    def total_counts(it):
        @pl.loop(1, n)
        def _(k):
            count_copy(it, k, lax.rem(z + n - k, n)).wait_recv()

        total = lax.fori_loop(1, n, lambda j, v: v + counts[it, j], counts[it, 0])
        return total[:, :1]

    def weighted(c):
        return jnp.dot(weights[...], fv[c], preferred_element_type=jnp.float32).astype(jnp.bfloat16)

    def placed(c):
        own = sv[:, pl.ds(pl.multiple_of(c * width, width), width)]
        return jnp.where(row // owned == z, jnp.concatenate([own] * n, axis=0), 0.0).astype(jnp.bfloat16)

    def picked(values):
        parts = [values[o * owned : (o + 1) * owned] for o in range(n)]
        return functools.reduce(lambda a, o: jnp.where(z == o, parts[o], a), range(1, n), parts[0])

    def combine_first(c, total):
        frame_copy(c).wait()
        score(c, total.astype(jnp.bfloat16))

    clear()
    sweep(0, placed, combine_first)
    for it in range(ITERS):
        expect(it)
        divisor = total_counts(it) + 1.0
        if it + 1 < ITERS:
            clear()

            def combine_next(c, total):
                score(c, ((total + model[c].astype(jnp.float32)) / divisor).astype(jnp.bfloat16))

            sweep(it + 1, weighted, combine_next)
        else:

            def combine_last(c, total):
                start = pl.multiple_of(c * width, width)
                new = (total + model[c].astype(jnp.float32)) / divisor
                out_ref[:, pl.ds(start, width)] = picked(new)

            sweep(it + 1, weighted, combine_last)

    for p in range(ITERS + 1):
        @pl.loop(0, n_chunks)
        def _(c):
            @pl.when(z < n - 1)
            def _():
                right_copy(p, c).wait_send()

            @pl.when(z > 0)
            def _():
                left_copy(p, c).wait_send()

    for it in range(ITERS):
        for k in range(1, group):
            raw_copy(it, k, me).wait_send()

        @pl.loop(1, n)
        def _(k):
            count_copy(it, k, z).wait_send()


def local(sizes, frames, slices, log_prior, orient):
    n, panels, subs = sizes
    group = panels * subs
    n_frames, pixels = frames.shape
    owned = slices.shape[0]
    rows = n * owned
    width = min(CHUNK, pixels)
    chunks = pixels // width
    passes = ITERS + 1
    bf, f32 = jnp.bfloat16, jnp.float32
    dma = pltpu.SemaphoreType.DMA
    return pl.pallas_call(
        functools.partial(kernel, sizes),
        out_shape=jax.ShapeDtypeStruct((owned, pixels), f32),
        in_specs=[
            pl.BlockSpec(memory_space=pl.ANY),
            pl.BlockSpec(memory_space=pl.ANY),
            pl.BlockSpec(memory_space=pltpu.SMEM),
            pl.BlockSpec(memory_space=pltpu.SMEM),
        ],
        out_specs=pl.BlockSpec(memory_space=pltpu.VMEM),
        scratch_shapes=[
            pltpu.VMEM((chunks, n_frames, width), bf),
            pltpu.VMEM((owned, pixels), f32),
            pltpu.VMEM((chunks, rows, width), bf),
            pltpu.VMEM((chunks, rows, width), bf),
            pltpu.VMEM((passes, chunks, rows, width), bf),
            pltpu.VMEM((passes, chunks, rows, width), bf),
            pltpu.VMEM((passes, chunks, rows, width), bf),
            pltpu.VMEM((passes, chunks, rows, width), bf),
            pltpu.VMEM((ITERS, group, rows, n_frames), f32),
            pltpu.VMEM((ITERS, n, rows, 128), f32),
            pltpu.VMEM((rows, n_frames), f32),
            pltpu.VMEM((rows, 1), f32),
            pltpu.VMEM((rows, n_frames), bf),
            dma((chunks,)),
            dma,
            dma((passes, chunks)),
            dma((passes, chunks)),
            dma((passes, chunks)),
            dma((passes, chunks)),
            dma((ITERS, group)),
            dma((ITERS, group)),
            dma((ITERS, n)),
            dma((ITERS, n)),
        ],
        compiler_params=pltpu.CompilerParams(
            collective_id=0, has_side_effects=True, vmem_limit_bytes=56 * 1024 * 1024
        ),
    )(frames, slices, log_prior, orient)


def solution(mesh):
    in_specs = (
        P(("groups", "frame"), ("panel", "sub")),
        P(("groups", "frame"), ("panel", "sub")),
        P(),
        P("groups"),
    )
    out_specs = P(("groups", "frame"), ("panel", "sub"))
    sizes = (mesh.shape["frame"], mesh.shape["panel"], mesh.shape["sub"])
    return jax.shard_map(
        functools.partial(local, sizes), mesh=mesh, in_specs=in_specs, out_specs=out_specs, check_vma=False
    )
```

```python
import functools
import math

import jax
import jax.numpy as jnp
from jax import lax
from jax.experimental import pallas as pl
from jax.experimental.pallas import tpu as pltpu
from jax.sharding import PartitionSpec as P

ITERS = 2
CHUNK = 1024
SKEW = 6
MESH = pl.DeviceIdType.MESH


def kernel(
    sizes, frames_ref, slices_ref, prior_ref, orient_ref, out_ref,
    fv, sv, model, gathered, sending, landed, term, from_left, from_right, to_right, to_left,
    raws, counts, raw_acc, norm_acc, weights, divisor,
    frame_sem, slice_sem, right_send, right_recv, left_send, left_recv,
    raw_send, raw_recv, count_send, count_recv,
    gather_send, gather_recv, owner_send, owner_recv,
):
    n, panels, subs = sizes
    group = panels * subs
    z = lax.axis_index("frame")
    me = lax.axis_index("panel") * subs + lax.axis_index("sub")
    n_chunks, n_frames, width = fv.shape
    owned = slices_ref.shape[0]
    rows = model.shape[1]
    groups, packed = gathered.shape[1:3]
    fold = packed // owned
    temper = 3.0 / math.sqrt(n_chunks * width * group)
    right, left = lax.rem(z + 1, n), lax.rem(z + n - 1, n)
    first, last = z == 0, z == n - 1

    slice_copy = pltpu.make_async_copy(slices_ref, sv, slice_sem)
    slice_copy.start()

    def frame_copy(c):
        start = pl.multiple_of(c * width, width)
        return pltpu.make_async_copy(frames_ref.at[:, pl.ds(start, width)], fv.at[c], frame_sem.at[c])

    @pl.loop(0, n_chunks)
    def _(c):
        frame_copy(c).start()

    def group_peer(k):
        other = lax.rem(me + k, group)
        return {"panel": other // subs, "sub": lax.rem(other, subs)}

    def frame_peer(k):
        return {"frame": lax.rem(z + k, n)}

    barrier = pltpu.get_barrier_semaphore()
    for k in range(1, group):
        pl.semaphore_signal(barrier, inc=1, device_id=group_peer(k), device_id_type=MESH)
    for k in range(1, n):
        pl.semaphore_signal(barrier, inc=1, device_id=frame_peer(k), device_id_type=MESH)

    slice_copy.wait()
    row = lax.broadcasted_iota(jnp.int32, (rows, 1), 0)
    prior = lax.fori_loop(
        0, rows, lambda m, v: jnp.where(row == m, prior_ref[orient_ref[m]], v), jnp.zeros((rows, 1), jnp.float32)
    )

    pl.semaphore_wait(barrier, group + n - 2)

    def right_copy(p, c):
        return pltpu.make_async_remote_copy(
            to_right.at[p, c], from_left.at[p, c], right_send.at[p, c], right_recv.at[p, c],
            device_id={"frame": right}, device_id_type=MESH,
        )

    def left_copy(p, c):
        return pltpu.make_async_remote_copy(
            to_left.at[p, c], from_right.at[p, c], left_send.at[p, c], left_recv.at[p, c],
            device_id={"frame": left}, device_id_type=MESH,
        )

    def raw_copy(it, k, slot):
        return pltpu.make_async_remote_copy(
            raws.at[it, me], raws.at[it, slot], raw_send.at[it, k], raw_recv.at[it, slot],
            device_id=group_peer(k), device_id_type=MESH,
        )

    def count_copy(it, k, slot):
        return pltpu.make_async_remote_copy(
            counts.at[it, z], counts.at[it, slot], count_send.at[it, k], count_recv.at[it, slot],
            device_id=frame_peer(k), device_id_type=MESH,
        )

    def sweep(p, make_term, combine):
        def step(s, _):
            @pl.when(s < n_chunks)
            def _():
                term[s] = make_term(s)

            c_right = s - z * SKEW

            @pl.when((c_right >= 0) & (c_right < n_chunks))
            def _():
                @pl.when(z > 0)
                def _():
                    right_copy(p, c_right).wait_recv()

                @pl.when(z < n - 1)
                def _():
                    came = jnp.where(first, 0.0, from_left[p, c_right].astype(jnp.float32))
                    to_right[p, c_right] = (came + term[c_right].astype(jnp.float32)).astype(jnp.bfloat16)
                    right_copy(p, c_right).start()

            c_left = s - (n - 1 - z) * SKEW

            @pl.when((c_left >= 0) & (c_left < n_chunks))
            def _():
                @pl.when(z < n - 1)
                def _():
                    left_copy(p, c_left).wait_recv()

                @pl.when(z > 0)
                def _():
                    came = jnp.where(last, 0.0, from_right[p, c_left].astype(jnp.float32))
                    to_left[p, c_left] = (came + term[c_left].astype(jnp.float32)).astype(jnp.bfloat16)
                    left_copy(p, c_left).start()

            c = s - jnp.maximum(z, n - 1 - z) * SKEW

            @pl.when((c >= 0) & (c < n_chunks))
            def _():
                low = jnp.where(first, 0.0, from_left[p, c].astype(jnp.float32))
                high = jnp.where(last, 0.0, from_right[p, c].astype(jnp.float32))
                combine(c, low + term[c].astype(jnp.float32) + high)

            return 0

        lax.fori_loop(0, n_chunks + (n - 1) * SKEW, step, 0)

    def score(c, rounded):
        model[c] = rounded
        wide = rounded.astype(jnp.float32)
        norm_acc[...] += jnp.sum(wide * wide, axis=1, keepdims=True)
        raw_acc[...] += lax.dot_general(
            rounded, fv[c], (((1,), (1,)), ((), ())), preferred_element_type=jnp.float32
        )

    def clear():
        raw_acc[...] = jnp.zeros_like(raw_acc)
        norm_acc[...] = jnp.zeros_like(norm_acc)

    def expect(it):
        raws[it, me] = raw_acc[...] - 0.5 * norm_acc[...]
        for k in range(1, group):
            raw_copy(it, k, me).start()
        for k in range(1, group):
            raw_copy(it, k, lax.rem(me + group - k, group)).wait_recv()
        summed = raws[it, 0]
        for j in range(1, group):
            summed = summed + raws[it, j]
        scores = temper * summed + prior
        top = jnp.exp(scores - jnp.max(scores, axis=0, keepdims=True))
        w = (top / jnp.sum(top, axis=0, keepdims=True)).astype(jnp.bfloat16)
        weights[...] = w
        mine = jnp.sum(w.astype(jnp.float32), axis=1, keepdims=True)
        counts[it, z] = jnp.broadcast_to(mine, counts.shape[2:])

        @pl.loop(1, n)
        def _(k):
            count_copy(it, k, z).start()

    def total_counts(it):
        @pl.loop(1, n)
        def _(k):
            count_copy(it, k, lax.rem(z + n - k, n)).wait_recv()

        total = lax.fori_loop(1, n, lambda j, v: v + counts[it, j], counts[it, 0])
        divisor[...] = total[:, :1] + 1.0

    def weighted(c):
        return jnp.dot(weights[...], fv[c], preferred_element_type=jnp.float32).astype(jnp.bfloat16)

    def picked(values):
        parts = [values[o * owned : (o + 1) * owned] for o in range(n)]
        return functools.reduce(lambda a, o: jnp.where(z == o, parts[o], a), range(1, n), parts[0])

    def columns(c):
        return pl.ds(pl.multiple_of(c * width, width), width)

    def gather_copy(g, k, slot):
        return pltpu.make_async_remote_copy(
            gathered.at[z, g], gathered.at[slot, g], gather_send.at[k, g], gather_recv.at[slot, g],
            device_id=frame_peer(k), device_id_type=MESH,
        )

    def owner_copy(g, k, slot):
        to = lax.rem(z + k, n)
        return pltpu.make_async_remote_copy(
            sending.at[to, g], landed.at[slot, g], owner_send.at[k, g], owner_recv.at[slot, g],
            device_id={"frame": to}, device_id_type=MESH,
        )

    def source(k):
        return lax.rem(z + n - k, n)

    @pl.loop(0, groups)
    def _(g):
        own = [sv[:, columns(g * fold + j)] for j in range(fold)]
        gathered[z, g] = jnp.concatenate(own, axis=0).astype(jnp.bfloat16)

        @pl.loop(1, n)
        def _(k):
            gather_copy(g, k, z).start()

    clear()

    @pl.loop(0, groups)
    def _(g):
        @pl.loop(1, n)
        def _(k):
            gather_copy(g, k, source(k)).wait_recv()

        blocks = [gathered[o, g].astype(jnp.float32) for o in range(n)]
        for j in range(fold):
            c = g * fold + j
            frame_copy(c).wait()
            whole = jnp.concatenate([b[j * owned : (j + 1) * owned] for b in blocks], axis=0)
            score(c, whole.astype(jnp.bfloat16))

    def last_update():
        @pl.loop(0, groups)
        def _(g):
            terms = [
                jnp.dot(weights[...], fv[g * fold + j], preferred_element_type=jnp.float32) for j in range(fold)
            ]
            for o in range(n):
                part = [t[o * owned : (o + 1) * owned] for t in terms]
                sending[o, g] = jnp.concatenate(part, axis=0).astype(jnp.bfloat16)

            @pl.loop(1, n)
            def _(k):
                owner_copy(g, k, z).start()

            landed[z, g] = sending[z, g]

        count_total()
        divide = jnp.concatenate([picked(divisor[...])] * fold, axis=0)

        @pl.loop(0, groups)
        def _(g):
            @pl.loop(1, n)
            def _(k):
                owner_copy(g, k, source(k)).wait_recv()

            own = [picked(model[g * fold + j].astype(jnp.float32)) for j in range(fold)]
            total = landed[0, g].astype(jnp.float32)
            for o in range(1, n):
                total = total + landed[o, g].astype(jnp.float32)
            new = (total + jnp.concatenate(own, axis=0)) / divide
            for j in range(fold):
                out_ref[:, columns(g * fold + j)] = new[j * owned : (j + 1) * owned]

    for it in range(ITERS):
        expect(it)

        def count_total():
            total_counts(it)

        if it + 1 < ITERS:
            clear()

            def combine_next(c, total):
                @pl.when(c == 0)
                def _():
                    count_total()

                score(c, ((total + model[c].astype(jnp.float32)) / divisor[...]).astype(jnp.bfloat16))

            sweep(it, weighted, combine_next)
        else:
            last_update()

    for p in range(ITERS - 1):
        @pl.loop(0, n_chunks)
        def _(c):
            @pl.when(z < n - 1)
            def _():
                right_copy(p, c).wait_send()

            @pl.when(z > 0)
            def _():
                left_copy(p, c).wait_send()

    for it in range(ITERS):
        for k in range(1, group):
            raw_copy(it, k, me).wait_send()

        @pl.loop(1, n)
        def _(k):
            count_copy(it, k, z).wait_send()

    @pl.loop(0, groups)
    def _(g):
        @pl.loop(1, n)
        def _(k):
            gather_copy(g, k, z).wait_send()
            owner_copy(g, k, z).wait_send()


def local(sizes, frames, slices, log_prior, orient):
    n, panels, subs = sizes
    group = panels * subs
    n_frames, pixels = frames.shape
    owned = slices.shape[0]
    rows = n * owned
    width = min(CHUNK, pixels)
    chunks = pixels // width
    passes = ITERS - 1
    fold = max(1, 16 // owned)
    groups = chunks // fold
    block = (n, groups, fold * owned, width)
    bf, f32 = jnp.bfloat16, jnp.float32
    dma = pltpu.SemaphoreType.DMA
    return pl.pallas_call(
        functools.partial(kernel, sizes),
        out_shape=jax.ShapeDtypeStruct((owned, pixels), f32),
        in_specs=[
            pl.BlockSpec(memory_space=pl.ANY),
            pl.BlockSpec(memory_space=pl.ANY),
            pl.BlockSpec(memory_space=pltpu.SMEM),
            pl.BlockSpec(memory_space=pltpu.SMEM),
        ],
        out_specs=pl.BlockSpec(memory_space=pltpu.VMEM),
        scratch_shapes=[
            pltpu.VMEM((chunks, n_frames, width), bf),
            pltpu.VMEM((owned, pixels), f32),
            pltpu.VMEM((chunks, rows, width), bf),
            pltpu.VMEM(block, bf),
            pltpu.VMEM(block, bf),
            pltpu.VMEM(block, bf),
            pltpu.VMEM((chunks, rows, width), bf),
            pltpu.VMEM((passes, chunks, rows, width), bf),
            pltpu.VMEM((passes, chunks, rows, width), bf),
            pltpu.VMEM((passes, chunks, rows, width), bf),
            pltpu.VMEM((passes, chunks, rows, width), bf),
            pltpu.VMEM((ITERS, group, rows, n_frames), f32),
            pltpu.VMEM((ITERS, n, rows, 128), f32),
            pltpu.VMEM((rows, n_frames), f32),
            pltpu.VMEM((rows, 1), f32),
            pltpu.VMEM((rows, n_frames), bf),
            pltpu.VMEM((rows, 1), f32),
            dma((chunks,)),
            dma,
            dma((passes, chunks)),
            dma((passes, chunks)),
            dma((passes, chunks)),
            dma((passes, chunks)),
            dma((ITERS, group)),
            dma((ITERS, group)),
            dma((ITERS, n)),
            dma((ITERS, n)),
            dma((n, groups)),
            dma((n, groups)),
            dma((n, groups)),
            dma((n, groups)),
        ],
        compiler_params=pltpu.CompilerParams(
            collective_id=0, has_side_effects=True, vmem_limit_bytes=56 * 1024 * 1024
        ),
    )(frames, slices, log_prior, orient)


def solution(mesh):
    in_specs = (
        P(("groups", "frame"), ("panel", "sub")),
        P(("groups", "frame"), ("panel", "sub")),
        P(),
        P("groups"),
    )
    out_specs = P(("groups", "frame"), ("panel", "sub"))
    sizes = (mesh.shape["frame"], mesh.shape["panel"], mesh.shape["sub"])
    return jax.shard_map(
        functools.partial(local, sizes), mesh=mesh, in_specs=in_specs, out_specs=out_specs, check_vma=False
    )
```

```python
import functools
import math

import jax
import jax.numpy as jnp
from jax import lax
from jax.experimental import pallas as pl
from jax.experimental.pallas import tpu as pltpu
from jax.sharding import PartitionSpec as P

ITERS = 2
CHUNK = 1024
SKEW = 5
PIECE = 1024
MESH = pl.DeviceIdType.MESH


def kernel(
    sizes, frames_ref, slices_ref, prior_hbm, orient_hbm, out_hbm,
    fv, sv, prior_ref, orient_ref, out_ref, prior_col, model, gathered, sending, landed, term, from_left, from_right, to_right, to_left,
    raws, counts, raw_acc, norm_acc, weights, divisor,
    frame_sem, slice_sem, prior_sem, orient_sem, out_sem, right_send, right_recv, left_send, left_recv,
    raw_send, raw_recv, count_send, count_recv,
    gather_send, gather_recv, owner_send, owner_recv,
):
    n, panels, subs = sizes
    group = panels * subs
    z = lax.axis_index("frame")
    me = lax.axis_index("panel") * subs + lax.axis_index("sub")
    n_chunks, n_frames, width = fv.shape
    owned = slices_ref.shape[0]
    rows = model.shape[1]
    groups, packed, piece = gathered.shape[1:]
    split = width // piece
    fold = packed // owned
    temper = 3.0 / math.sqrt(n_chunks * width * group)
    right, left = lax.rem(z + 1, n), lax.rem(z + n - 1, n)
    first, last = z == 0, z == n - 1

    slice_copy = pltpu.make_async_copy(slices_ref, sv, slice_sem)
    slice_copy.start()
    prior_copy = pltpu.make_async_copy(prior_hbm, prior_ref, prior_sem)
    prior_copy.start()
    orient_copy = pltpu.make_async_copy(orient_hbm, orient_ref, orient_sem)
    orient_copy.start()

    def frame_copy(c):
        start = pl.multiple_of(c * width, width)
        return pltpu.make_async_copy(frames_ref.at[:, pl.ds(start, width)], fv.at[c], frame_sem.at[c])

    @pl.loop(0, n_chunks)
    def _(c):
        frame_copy(c).start()

    def group_peer(k):
        other = lax.rem(me + k, group)
        return {"panel": other // subs, "sub": lax.rem(other, subs)}

    def frame_peer(k):
        return {"frame": lax.rem(z + k, n)}

    barrier = pltpu.get_barrier_semaphore()
    for k in range(1, group):
        pl.semaphore_signal(barrier, inc=1, device_id=group_peer(k), device_id_type=MESH)
    for k in range(1, n):
        pl.semaphore_signal(barrier, inc=1, device_id=frame_peer(k), device_id_type=MESH)

    def group_columns(g, j):
        return pl.ds(pl.multiple_of(g * (fold * piece) + j * piece, piece), piece)

    def part_frames(g, j):
        return fv[g * fold // split + j // split, :, j % split * piece : (j % split + 1) * piece]

    slice_copy.wait()

    @pl.loop(0, groups)
    def _(g):
        own = [sv[:, group_columns(g, j)] for j in range(fold)]
        gathered[z, g] = jnp.concatenate(own, axis=0).astype(jnp.bfloat16)

    pl.semaphore_wait(barrier, group + n - 2)

    def right_copy(p, c):
        return pltpu.make_async_remote_copy(
            to_right.at[p, c], from_left.at[p, c], right_send.at[p, c], right_recv.at[p, c],
            device_id={"frame": right}, device_id_type=MESH,
        )

    def left_copy(p, c):
        return pltpu.make_async_remote_copy(
            to_left.at[p, c], from_right.at[p, c], left_send.at[p, c], left_recv.at[p, c],
            device_id={"frame": left}, device_id_type=MESH,
        )

    def raw_copy(it, k, slot):
        return pltpu.make_async_remote_copy(
            raws.at[it, me], raws.at[it, slot], raw_send.at[it, k], raw_recv.at[it, slot],
            device_id=group_peer(k), device_id_type=MESH,
        )

    def count_copy(it, k, slot):
        return pltpu.make_async_remote_copy(
            counts.at[it, z], counts.at[it, slot], count_send.at[it, k], count_recv.at[it, slot],
            device_id=frame_peer(k), device_id_type=MESH,
        )

    def sweep(p, make_term, combine):
        def step(s, _):
            @pl.when(s < n_chunks)
            def _():
                term[s] = make_term(s)

            c_right = s - z * SKEW

            @pl.when((c_right >= 0) & (c_right < n_chunks))
            def _():
                @pl.when(z > 0)
                def _():
                    right_copy(p, c_right).wait_recv()

                @pl.when(z < n - 1)
                def _():
                    came = jnp.where(first, 0.0, from_left[p, c_right].astype(jnp.float32))
                    to_right[p, c_right] = (came + term[c_right].astype(jnp.float32)).astype(jnp.bfloat16)
                    right_copy(p, c_right).start()

            c_left = s - (n - 1 - z) * SKEW

            @pl.when((c_left >= 0) & (c_left < n_chunks))
            def _():
                @pl.when(z < n - 1)
                def _():
                    left_copy(p, c_left).wait_recv()

                @pl.when(z > 0)
                def _():
                    came = jnp.where(last, 0.0, from_right[p, c_left].astype(jnp.float32))
                    to_left[p, c_left] = (came + term[c_left].astype(jnp.float32)).astype(jnp.bfloat16)
                    left_copy(p, c_left).start()

            c = s - jnp.maximum(z, n - 1 - z) * SKEW

            @pl.when((c >= 0) & (c < n_chunks))
            def _():
                low = jnp.where(first, 0.0, from_left[p, c].astype(jnp.float32))
                high = jnp.where(last, 0.0, from_right[p, c].astype(jnp.float32))
                combine(c, low + term[c].astype(jnp.float32) + high)

            return 0

        lax.fori_loop(0, n_chunks + (n - 1) * SKEW, step, 0)

    def score(rounded, frames):
        wide = rounded.astype(jnp.float32)
        norm_acc[...] += jnp.sum(wide * wide, axis=1, keepdims=True)
        raw_acc[...] += lax.dot_general(
            rounded, frames, (((1,), (1,)), ((), ())), preferred_element_type=jnp.float32
        )

    def clear():
        raw_acc[...] = jnp.zeros_like(raw_acc)
        norm_acc[...] = jnp.zeros_like(norm_acc)

    def expect(it):
        raws[it, me] = raw_acc[...] - 0.5 * norm_acc[...]
        for k in range(1, group):
            raw_copy(it, k, me).start()
        for k in range(1, group):
            raw_copy(it, k, lax.rem(me + group - k, group)).wait_recv()
        summed = raws[it, 0]
        for j in range(1, group):
            summed = summed + raws[it, j]
        scores = temper * summed + prior_col[...]
        top = jnp.exp(scores - jnp.max(scores, axis=0, keepdims=True))
        w = (top / jnp.sum(top, axis=0, keepdims=True)).astype(jnp.bfloat16)
        weights[...] = w
        mine = jnp.sum(w.astype(jnp.float32), axis=1, keepdims=True)
        counts[it, z] = jnp.broadcast_to(mine, counts.shape[2:])

        @pl.loop(1, n)
        def _(k):
            count_copy(it, k, z).start()

    def total_counts(it):
        @pl.loop(1, n)
        def _(k):
            count_copy(it, k, lax.rem(z + n - k, n)).wait_recv()

        total = lax.fori_loop(1, n, lambda j, v: v + counts[it, j], counts[it, 0])
        divisor[...] = total[:, :1] + 1.0

    def weighted(c):
        return jnp.dot(weights[...], fv[c], preferred_element_type=jnp.float32).astype(jnp.bfloat16)

    def picked(values):
        parts = [values[o * owned : (o + 1) * owned] for o in range(n)]
        return functools.reduce(lambda a, o: jnp.where(z == o, parts[o], a), range(1, n), parts[0])

    def gather_copy(g, k, slot):
        return pltpu.make_async_remote_copy(
            gathered.at[z, g], gathered.at[slot, g], gather_send.at[k, g], gather_recv.at[slot, g],
            device_id=frame_peer(k), device_id_type=MESH,
        )

    def owner_copy(g, k, slot):
        to = lax.rem(z + k, n)
        return pltpu.make_async_remote_copy(
            sending.at[to, g], landed.at[slot, g], owner_send.at[k, g], owner_recv.at[slot, g],
            device_id={"frame": to}, device_id_type=MESH,
        )

    def source(k):
        return lax.rem(z + n - k, n)

    @pl.loop(0, groups)
    def _(g):
        @pl.loop(1, n)
        def _(k):
            gather_copy(g, k, z).start()

    clear()
    prior_copy.wait()
    orient_copy.wait()
    row = lax.broadcasted_iota(jnp.int32, (rows, 1), 0)
    prior_col[...] = lax.fori_loop(
        0, rows, lambda m, v: jnp.where(row == m, prior_ref[orient_ref[m]], v), jnp.zeros((rows, 1), jnp.float32)
    )

    @pl.loop(0, groups)
    def _(g):
        @pl.loop(1, n)
        def _(k):
            gather_copy(g, k, source(k)).wait_recv()

        blocks = [gathered[o, g].astype(jnp.float32) for o in range(n)]
        for j in range(fold // split):
            frame_copy(g * fold // split + j).wait()
        for j in range(fold):
            whole = jnp.concatenate([b[j * owned : (j + 1) * owned] for b in blocks], axis=0).astype(jnp.bfloat16)
            model[g * fold // split + j // split, :, j % split * piece : (j % split + 1) * piece] = whole
            score(whole, part_frames(g, j))

    def out_copy(g):
        span = pl.ds(pl.multiple_of(g * (fold * piece), fold * piece), fold * piece)
        return pltpu.make_async_copy(out_ref.at[:, span], out_hbm.at[:, span], out_sem.at[g])

    def last_update():
        @pl.loop(0, groups)
        def _(g):
            terms = [
                jnp.dot(weights[...], part_frames(g, j), preferred_element_type=jnp.float32) for j in range(fold)
            ]
            for o in range(n):
                part = [t[o * owned : (o + 1) * owned] for t in terms]
                sending[o, g] = jnp.concatenate(part, axis=0).astype(jnp.bfloat16)

            @pl.loop(1, n)
            def _(k):
                owner_copy(g, k, z).start()

            landed[z, g] = sending[z, g]

        count_total()
        divide = jnp.concatenate([picked(divisor[...])] * fold, axis=0)

        @pl.loop(0, groups)
        def _(g):
            @pl.loop(1, n)
            def _(k):
                owner_copy(g, k, source(k)).wait_recv()

            held = [model[g * fold // split + c] for c in range(fold // split)]
            own = [
                picked(held[j // split][:, j % split * piece : (j % split + 1) * piece].astype(jnp.float32))
                for j in range(fold)
            ]
            total = landed[0, g].astype(jnp.float32)
            for o in range(1, n):
                total = total + landed[o, g].astype(jnp.float32)
            new = (total + jnp.concatenate(own, axis=0)) / divide
            for j in range(fold):
                out_ref[:, group_columns(g, j)] = new[j * owned : (j + 1) * owned]
            out_copy(g).start()

        @pl.loop(0, groups)
        def _(g):
            out_copy(g).wait()

    for it in range(ITERS):
        expect(it)

        def count_total():
            total_counts(it)

        if it + 1 < ITERS:
            clear()

            def combine_next(c, total):
                @pl.when(c == 0)
                def _():
                    count_total()

                rounded = ((total + model[c].astype(jnp.float32)) / divisor[...]).astype(jnp.bfloat16)
                model[c] = rounded
                score(rounded, fv[c])

            sweep(it, weighted, combine_next)
        else:
            last_update()

    for p in range(ITERS - 1):
        @pl.loop(0, n_chunks)
        def _(c):
            @pl.when(z < n - 1)
            def _():
                right_copy(p, c).wait_send()

            @pl.when(z > 0)
            def _():
                left_copy(p, c).wait_send()

    for it in range(ITERS):
        for k in range(1, group):
            raw_copy(it, k, me).wait_send()

        @pl.loop(1, n)
        def _(k):
            count_copy(it, k, z).wait_send()

    @pl.loop(0, groups)
    def _(g):
        @pl.loop(1, n)
        def _(k):
            gather_copy(g, k, z).wait_send()
            owner_copy(g, k, z).wait_send()


def local(sizes, frames, slices, log_prior, orient):
    n, panels, subs = sizes
    group = panels * subs
    n_frames, pixels = frames.shape
    owned = slices.shape[0]
    rows = n * owned
    width = min(CHUNK, pixels)
    chunks = pixels // width
    passes = ITERS - 1
    fold = max(1, 16 // owned)
    piece = min(PIECE, width)
    groups = pixels // (fold * piece)
    block = (n, groups, fold * owned, piece)
    bf, f32 = jnp.bfloat16, jnp.float32
    dma = pltpu.SemaphoreType.DMA
    return pl.pallas_call(
        functools.partial(kernel, sizes),
        out_shape=jax.ShapeDtypeStruct((owned, pixels), f32),
        in_specs=[
            pl.BlockSpec(memory_space=pl.ANY),
            pl.BlockSpec(memory_space=pl.ANY),
            pl.BlockSpec(memory_space=pl.ANY),
            pl.BlockSpec(memory_space=pl.ANY),
        ],
        out_specs=pl.BlockSpec(memory_space=pl.ANY),
        scratch_shapes=[
            pltpu.VMEM((chunks, n_frames, width), bf),
            pltpu.VMEM((owned, pixels), f32),
            pltpu.SMEM(log_prior.shape, f32),
            pltpu.SMEM(orient.shape, jnp.int32),
            pltpu.VMEM((owned, pixels), f32),
            pltpu.VMEM((rows, 1), f32),
            pltpu.VMEM((chunks, rows, width), bf),
            pltpu.VMEM(block, bf),
            pltpu.VMEM(block, bf),
            pltpu.VMEM(block, bf),
            pltpu.VMEM((chunks, rows, width), bf),
            pltpu.VMEM((passes, chunks, rows, width), bf),
            pltpu.VMEM((passes, chunks, rows, width), bf),
            pltpu.VMEM((passes, chunks, rows, width), bf),
            pltpu.VMEM((passes, chunks, rows, width), bf),
            pltpu.VMEM((ITERS, group, rows, n_frames), f32),
            pltpu.VMEM((ITERS, n, rows, 128), f32),
            pltpu.VMEM((rows, n_frames), f32),
            pltpu.VMEM((rows, 1), f32),
            pltpu.VMEM((rows, n_frames), bf),
            pltpu.VMEM((rows, 1), f32),
            dma((chunks,)),
            dma,
            dma,
            dma,
            dma((groups,)),
            dma((passes, chunks)),
            dma((passes, chunks)),
            dma((passes, chunks)),
            dma((passes, chunks)),
            dma((ITERS, group)),
            dma((ITERS, group)),
            dma((ITERS, n)),
            dma((ITERS, n)),
            dma((n, groups)),
            dma((n, groups)),
            dma((n, groups)),
            dma((n, groups)),
        ],
        compiler_params=pltpu.CompilerParams(
            collective_id=0, has_side_effects=True, vmem_limit_bytes=56 * 1024 * 1024
        ),
    )(frames, slices, log_prior, orient)


def solution(mesh):
    in_specs = (
        P(("groups", "frame"), ("panel", "sub")),
        P(("groups", "frame"), ("panel", "sub")),
        P(),
        P("groups"),
    )
    out_specs = P(("groups", "frame"), ("panel", "sub"))
    sizes = (mesh.shape["frame"], mesh.shape["panel"], mesh.shape["sub"])
    return jax.shard_map(
        functools.partial(local, sizes), mesh=mesh, in_specs=in_specs, out_specs=out_specs, check_vma=False
    )
```
